128 devices in a mesh: queue: 64 (over y, z_hi, x, core), tp: 2 (over z_lo).
Axes of the slice: x: 4, y: 4, z: 4 (z_hi: 2, z_lo: 2; z = z_hi * 2 + z_lo), core: 2. Of those that a mesh axis runs over, the one named last changes fastest.
Arguments:
- latent: bfloat16 [64, 128, 3072], P('queue', None, 'tp'), may hold values from -6 to 6
- step_index: int32 [64], P('queue'), may hold values from 0 to 49
- back_reach: int32 [64], P('queue'), may hold values from 1 to 2
- ahead_reach: int32 [64], P('queue'), may hold values from 1 to 2
- level_mod: float32 [50, 2, 3072], replicated, may hold values from -20 to 20
- text_mod: float32 [2, 2, 3072], replicated, may hold values from -3 to 3
- w_qkv: bfloat16 [3, 3072, 1536], P(None, None, 'tp'), may hold values from -0.109375 to 0.109375
- w_out: bfloat16 [1536, 3072], P('tp'), may hold values from -0.15625 to 0.15625
- keep_coef: float32 [50], replicated, may hold values from 0.6 to 1
- noise_coef: float32 [50], replicated, may hold values from 0.2 to 1
Outputs:
- rolled: bfloat16 [64, 128, 3072], P('queue', None, 'tp')
The draws below stay inside these ranges and needn't reach their ends.
All inputs are finite; a program needn't handle non-finite values.
Results may differ from the reference program's by a relative error of at most 0.012.
The reference program's roundings to bfloat16 on the way (of `normed`, `probs`, `attended` and `renewed`) count: a program that leaves them out, or rounds other values in their place, can miss the bound.
Values may be sent and summed in bfloat16 or wider, within the bound.
No kernel may reach another device: no remote copies, remote signals or barrier semaphores. Data moves between devices by JAX's collectives and lax.ppermute only.
A program may use at most 128 MiB of HBM per device.

```python
import math
import jax
import jax.numpy as jnp
from jax import lax

D = 3072
HEADS = 24
HDIM = 64
S = 128
LEVELS = 50
REACH = 2
FRAMES = 64


def draw_level_mod(key, part):
    key_shift = jax.random.fold_in(key, 11)
    key_scale = jax.random.fold_in(key, 12)
    shift_terms = 0.3 * jax.random.normal(key_shift, (LEVELS, D), jnp.float32)
    scale_terms = 0.3 * jax.random.normal(key_scale, (LEVELS, D), jnp.float32)
    shift_terms = jnp.clip(shift_terms, -20.0, 20.0)
    scale_terms = jnp.clip(scale_terms, -20.0, 20.0)
    return jnp.stack([shift_terms, scale_terms], axis=1)


def touch_ends(result, key, smallest, top_value):
    dims = result.shape
    spot = [jax.random.randint(jax.random.fold_in(key, axis), (), 0, dims[axis]) for axis in range(len(dims))]
    result = result.at[tuple(spot)].set(smallest)
    longest = dims.index(max(dims))
    spot[longest] = (spot[longest] + 1) % dims[longest]
    return result.at[tuple(spot)].set(top_value)


def level_of(stream_key, extent, cuts, smallest, high):
    level = 1.0
    for dim, parts in cuts:
        heights = jax.random.uniform(jax.random.fold_in(jax.random.fold_in(stream_key, 6), dim), (parts,), jnp.float32, smallest / len(cuts), high / len(cuts))
        level = level * jnp.repeat(jnp.exp(heights), extent[dim] // parts).reshape((-1,) + (1,) * (len(extent) - 1 - dim))
    return level


def noise(stream_key, extent, scale, bound, split=(), kind=jnp.bfloat16):
    entries = scale * jax.random.normal(stream_key, extent, jnp.float32)
    if split:
        entries = entries * level_of(stream_key, extent, split, -0.22, 0.18)
    return jnp.clip(entries, -bound, bound).astype(kind)


def setup_inputs(seed: int = 0) -> dict:
    arg_keys = jax.random.split(jax.random.key(seed), 11)
    return {
        "latent": noise(arg_keys[0], (FRAMES, S, D), 1.0, 6.0, ((0, 64), (2, 2))),
        "step_index": touch_ends(jax.random.randint(arg_keys[1], (FRAMES,), 0, LEVELS), jax.random.fold_in(arg_keys[1], 1), 0, LEVELS - 1).astype(jnp.int32),
        "back_reach": touch_ends(jax.random.randint(arg_keys[2], (FRAMES,), 1, REACH + 1), jax.random.fold_in(arg_keys[2], 1), 1, REACH).astype(jnp.int32),
        "ahead_reach": touch_ends(jax.random.randint(arg_keys[3], (FRAMES,), 1, REACH + 1), jax.random.fold_in(arg_keys[3], 1), 1, REACH).astype(jnp.int32),
        "level_mod": draw_level_mod(jax.random.fold_in(arg_keys[10], 71), 0),
        "text_mod": noise(arg_keys[5], (2, 2, D), 0.5, 3.0, (), jnp.float32),
        "w_qkv": noise(arg_keys[6], (3, D, HEADS * HDIM), D ** -0.5, 0.109375, ((2, 2),)),
        "w_out": noise(arg_keys[7], (HEADS * HDIM, D), (HEADS * HDIM) ** -0.5, 0.15625, ((0, 2),)),
        "keep_coef": jnp.clip(jax.random.uniform(arg_keys[8], (LEVELS,), jnp.float32, 0.6, 1.0), 0.6, 1.0),
        "noise_coef": jnp.clip(jnp.exp(jax.random.uniform(arg_keys[9], (LEVELS,), jnp.float32, math.log(0.2), math.log(1.0))), 0.2, 1.0),
    }


epsilon = 1e-06
guidance = 6.0

def reference(latent, step_index, back_reach, ahead_reach, level_mod, text_mod, w_qkv, w_out, keep_coef, noise_coef):
    frames = latent.shape[0]
    tokens = latent.shape[1]
    gathered = latent.astype(jnp.float32)
    row_mean = lax.optimization_barrier(jnp.mean(gathered, axis=-1, keepdims=True))
    centred = gathered - row_mean
    spread = lax.optimization_barrier(jnp.mean(centred * centred, axis=-1, keepdims=True))
    unit_rows = centred * lax.rsqrt(spread + epsilon)
    modulation = level_mod[step_index]
    shift_terms = modulation[:, 0][:, None, :] + text_mod[None, :, 0]
    scale_terms = modulation[:, 1][:, None, :] + text_mod[None, :, 1]
    normed = (unit_rows[:, None] * (1.0 + scale_terms[:, :, None, :]) + shift_terms[:, :, None, :]).astype(jnp.bfloat16)
    flat = normed.reshape(frames * 2 * tokens, D)
    queries = jnp.dot(flat, w_qkv[0], preferred_element_type=jnp.float32).astype(jnp.bfloat16)
    key_rows = jnp.dot(flat, w_qkv[1], preferred_element_type=jnp.float32).astype(jnp.bfloat16)
    value_rows = jnp.dot(flat, w_qkv[2], preferred_element_type=jnp.float32).astype(jnp.bfloat16)
    queries = queries.reshape(frames, 2, tokens, HEADS, HDIM)
    key_rows = key_rows.reshape(frames, 2, tokens, HEADS, HDIM)
    value_rows = value_rows.reshape(frames, 2, tokens, HEADS, HDIM)
    padding = ((REACH, REACH), (0, 0), (0, 0), (0, 0), (0, 0))
    keys_padded = jnp.pad(key_rows, padding)
    values_padded = jnp.pad(value_rows, padding)
    offsets = jnp.arange(-REACH, REACH + 1, dtype=jnp.int32)
    span = 2 * REACH + 1

    def attend(frame_at):
        key_window = lax.dynamic_slice_in_dim(keys_padded, frame_at, span, 0)
        value_window = lax.dynamic_slice_in_dim(values_padded, frame_at, span, 0)
        key_window = jnp.transpose(key_window, (1, 0, 2, 3, 4)).reshape(2, span * tokens, HEADS, HDIM)
        value_window = jnp.transpose(value_window, (1, 0, 2, 3, 4)).reshape(2, span * tokens, HEADS, HDIM)
        back_now = lax.dynamic_index_in_dim(back_reach, frame_at, 0, keepdims=False)
        ahead_now = lax.dynamic_index_in_dim(ahead_reach, frame_at, 0, keepdims=False)
        target = frame_at + offsets
        allowed = (offsets >= -back_now) & (offsets <= ahead_now) & (target >= 0) & (target < frames)
        key_mask = jnp.repeat(allowed, tokens)
        query_now = lax.dynamic_index_in_dim(queries, frame_at, 0, keepdims=False)
        scores = jnp.einsum('bshd,bkhd->bhsk', query_now.astype(jnp.float32), key_window.astype(jnp.float32)) * HDIM ** (-0.5)
        scores = jnp.where(key_mask[None, None, None, :], scores, -1e+30)
        top = lax.optimization_barrier(jnp.max(scores, axis=-1, keepdims=True))
        expon = jnp.exp(scores - top)
        probs = (expon / lax.optimization_barrier(jnp.sum(expon, axis=-1, keepdims=True))).astype(jnp.bfloat16)
        attended = jnp.einsum('bhsk,bkhd->bshd', probs.astype(jnp.float32), value_window.astype(jnp.float32))
        return attended.astype(jnp.bfloat16).reshape(2, tokens, HEADS * HDIM)
    attended = lax.map(attend, jnp.arange(frames, dtype=jnp.int32))
    predicted = jnp.dot(attended.reshape(frames * 2 * tokens, HEADS * HDIM), w_out, preferred_element_type=jnp.float32)
    predicted = predicted.reshape(frames, 2, tokens, D)
    guided = predicted[:, 1] + guidance * (predicted[:, 0] - predicted[:, 1])
    keep_now = keep_coef[step_index][:, None, None]
    noise_now = noise_coef[step_index][:, None, None]
    renewed = (keep_now * gathered - noise_now * guided).astype(jnp.bfloat16)
    return jnp.roll(renewed, 1, axis=0)
```

```python
import functools

import jax
import jax.numpy as jnp
from jax import lax
from jax.experimental import pallas as pl
from jax.experimental.pallas import tpu as pltpu
from jax.sharding import PartitionSpec as P

HDIM = 64
GROUPS = 3
EPSILON = 1e-06
GUIDANCE = 6.0
F32 = jnp.float32
BF16 = jnp.bfloat16
VMEM = pltpu.VMEM
LIMIT = pltpu.CompilerParams(vmem_limit_bytes=16 << 20)


def norm_kernel(info, native, foreign, level, text, out):
    tokens, half = native.shape
    side = info[3]
    total = 2 * half
    parts = (native[...].astype(F32), foreign[...].astype(F32))
    mean = sum(jnp.sum(p, axis=-1, keepdims=True) for p in parts) / total
    parts = tuple(p - mean for p in parts)
    spread = sum(jnp.sum(p * p, axis=-1, keepdims=True) for p in parts) / total
    inverse = lax.rsqrt(spread + EPSILON)
    for part, which in zip(parts, (side, 1 - side)):
        unit = part * inverse
        cols = pl.ds(pl.multiple_of(which * half, half), half)
        for branch in range(2):
            shift = level[0, 0:1, cols] + text[branch, 0:1, cols]
            scale = level[0, 1:2, cols] + text[branch, 1:2, cols]
            out[branch * tokens : (branch + 1) * tokens, cols] = (unit * (1.0 + scale) + shift).astype(BF16)


def normalize(info, native, foreign, level_mod, text_mod):
    tokens, half = native.shape
    full = 2 * half
    whole = lambda shape: pl.BlockSpec(shape, lambda i, info: (0,) * len(shape))
    return pl.pallas_call(
        norm_kernel,
        out_shape=jax.ShapeDtypeStruct((2 * tokens, full), BF16),
        grid_spec=pltpu.PrefetchScalarGridSpec(
            num_scalar_prefetch=1,
            grid=(1,),
            in_specs=[
                whole((tokens, half)),
                whole((tokens, half)),
                pl.BlockSpec((1, 2, full), lambda i, info: (info[0], 0, 0)),
                whole((2, 2, full)),
            ],
            out_specs=whole((2 * tokens, full)),
        ),
        cost_estimate=pl.CostEstimate(flops=10 * tokens * full, bytes_accessed=6 * tokens * full, transcendentals=0),
        compiler_params=LIMIT,
        name="norm",
    )(info, native, foreign, level_mod, text_mod)


def project_kernel(x, w, out):
    out[0] = jnp.dot(x[...], w[0], preferred_element_type=F32).astype(BF16)


def project(x, w_qkv, first, count, group, width, name):
    rows, depth = x.shape
    return pl.pallas_call(
        project_kernel,
        out_shape=jax.ShapeDtypeStruct((count, rows, width), BF16),
        grid=(count,),
        in_specs=[
            pl.BlockSpec((rows, depth), lambda i: (0, 0)),
            pl.BlockSpec((1, depth, width), lambda i: (first + i, 0, group)),
        ],
        out_specs=pl.BlockSpec((1, rows, width), lambda i: (i, 0, 0)),
        cost_estimate=pl.CostEstimate(
            flops=2 * count * rows * depth * width,
            bytes_accessed=2 * (count * depth * width + rows * depth),
            transcendentals=0,
        ),
        compiler_params=LIMIT,
        name=name,
    )(x, w_qkv)


def attend_kernel(bias, q, *refs):
    *blocks, out = refs
    rows, width = q.shape[1:]
    tokens = rows // 2
    heads = width // HDIM
    lane_head = lax.broadcasted_iota(jnp.int32, (1, width), 1) // HDIM
    results = []
    for branch in range(2):
        at = slice(branch * tokens, (branch + 1) * tokens)
        keys = jnp.concatenate([block[0, at, :] for block in blocks], axis=0)
        values = jnp.concatenate([block[1, at, :] for block in blocks], axis=0)
        query = q[0, at, :] * jnp.asarray(HDIM ** (-0.5), BF16)
        stacked = jnp.concatenate(
            [jnp.where(lane_head == h, query, jnp.zeros_like(query)) for h in range(heads)], axis=0
        )
        scores = lax.dot_general(stacked, keys, (((1,), (1,)), ((), ())), preferred_element_type=F32)
        scores = jnp.concatenate(
            [scores[:, i * tokens : (i + 1) * tokens] + bias[i] for i in range(len(blocks))], axis=1
        )
        top = jnp.max(scores, axis=-1, keepdims=True)
        expon = jnp.exp(scores - top)
        probs = (expon * (1.0 / jnp.sum(expon, axis=-1, keepdims=True))).astype(BF16)
        mixed = jnp.dot(probs, values, preferred_element_type=F32)
        picked = mixed[0:tokens]
        for h in range(1, heads):
            picked = jnp.where(lane_head == h, mixed[h * tokens : (h + 1) * tokens], picked)
        results.append(picked.astype(BF16).astype(F32))
    cond, plain = results
    out[...] = (plain + GUIDANCE * (cond - plain)).astype(BF16)


def attend(bias, q, blocks, name):
    _, rows, width = q.shape
    tokens = rows // 2
    heads = width // HDIM
    keys = tokens * len(blocks)
    return pl.pallas_call(
        attend_kernel,
        out_shape=jax.ShapeDtypeStruct((tokens, width), BF16),
        in_specs=[pl.BlockSpec(memory_space=pltpu.SMEM)] + [pl.BlockSpec(memory_space=VMEM)] * (1 + len(blocks)),
        out_specs=pl.BlockSpec(memory_space=VMEM),
        cost_estimate=pl.CostEstimate(
            flops=8 * heads * tokens * keys * width,
            bytes_accessed=8 * keys * width,
            transcendentals=2 * heads * tokens * keys,
        ),
        compiler_params=LIMIT,
        name=name,
    )(bias, q, *blocks)


def out_kernel(side, *refs):
    *mixes, w, out = refs
    width = mixes[0].shape[1]
    total = None
    for i, mix in enumerate(mixes):
        term = jnp.dot(mix[...], w[i * width : (i + 1) * width, :], preferred_element_type=F32)
        total = term if total is None else total + term
    out[...] = total.astype(out.dtype)


def project_out(side, mixes, w_out, dtype, name):
    tokens, width = mixes[0].shape
    depth, full = w_out.shape
    half = full // 2
    step = 512
    steps = half // step
    return pl.pallas_call(
        out_kernel,
        out_shape=jax.ShapeDtypeStruct((tokens, half), dtype),
        grid_spec=pltpu.PrefetchScalarGridSpec(
            num_scalar_prefetch=1,
            grid=(steps,),
            in_specs=[pl.BlockSpec((tokens, width), lambda i, side: (0, 0))] * len(mixes)
            + [pl.BlockSpec((depth, step), lambda i, side: (0, side[0] * steps + i))],
            out_specs=pl.BlockSpec((tokens, step), lambda i, side: (0, i)),
        ),
        cost_estimate=pl.CostEstimate(
            flops=2 * tokens * depth * half, bytes_accessed=2 * depth * half, transcendentals=0
        ),
        compiler_params=LIMIT,
        name=name,
    )(side, *mixes, w_out)


def on_device(
    latent,
    step_index,
    back_reach,
    ahead_reach,
    level_mod,
    text_mod,
    w_qkv,
    w_out,
    keep_coef,
    noise_coef,
):
    count = lax.axis_size("queue")
    slot = lax.axis_index("queue")
    side = lax.axis_index("tp")
    frame = lax.rem(slot + count - 1, count)
    every = range(count)
    onward = [(s, (s + 1) % count) for s in every]
    across = [(2 * s + t, 2 * ((s + 1) % count) + 1 - t) for s in every for t in range(2)]
    mates = [(s, s ^ 1) for s in every]
    near = [(s, (s + 1) % count if s % 2 else (s - 1) % count) for s in every]
    far = [(s, (s - 2) % count if s % 2 else (s + 2) % count) for s in every]

    foreign = lax.ppermute(latent[0], ("queue", "tp"), across)
    native = lax.ppermute(latent[0], "queue", onward)
    facts = lax.ppermute(jnp.concatenate([step_index, back_reach, ahead_reach]), "queue", onward)
    step, back, ahead = facts[0], facts[1], facts[2]
    info = jnp.concatenate([facts, side[None]])

    normed = normalize(info, native, foreign, level_mod, text_mod)
    width = w_qkv.shape[2] // GROUPS

    sense = jnp.where(slot % 2 == 0, 1, -1)
    offsets = jnp.stack([0 * sense, sense, -sense, -2 * sense, 2 * sense])
    target = frame + offsets
    allowed = (offsets >= -back) & (offsets <= ahead) & (target >= 0) & (target < count)
    bias = jnp.where(allowed, 0.0, -1e30).astype(F32)

    own, mate, close, distant = [], [], [], []
    for g in range(GROUPS):
        kv = project(normed, w_qkv, 1, 2, g, width, "kv%d" % g)
        own.append(kv)
        close.append(lax.ppermute(kv, "queue", near))
        distant.append(lax.ppermute(kv, "queue", far))
        mate.append(lax.ppermute(kv, "queue", mates))
    mixes = []
    for g in range(GROUPS):
        q = project(normed, w_qkv, 0, 1, g, width, "q%d" % g)
        passed = lax.ppermute(close[g], "queue", mates)
        mixes.append(attend(bias, q, [own[g], mate[g], close[g], distant[g], passed], "attend%d" % g))

    swap = [(0, 1), (1, 0)]
    theirs = project_out(1 - side[None], mixes, w_out, BF16, "out_theirs")
    received = lax.ppermute(theirs, "tp", swap)
    ours = project_out(side[None], mixes, w_out, F32, "out_ours")
    keep_now = lax.dynamic_index_in_dim(keep_coef, step, 0, keepdims=False)
    noise_now = lax.dynamic_index_in_dim(noise_coef, step, 0, keepdims=False)
    guided = ours + received.astype(F32)
    return (keep_now * native.astype(F32) - noise_now * guided).astype(BF16)[None]


def solution(mesh):
    return jax.shard_map(
        on_device,
        mesh=mesh,
        in_specs=(
            P("queue", None, "tp"),
            P("queue"),
            P("queue"),
            P("queue"),
            P(),
            P(),
            P(None, None, "tp"),
            P("tp", None),
            P(),
            P(),
        ),
        out_specs=P("queue", None, "tp"),
        check_vma=False,
    )
```

```python
import jax
import jax.numpy as jnp
from jax import lax
from jax.experimental import pallas as pl
from jax.experimental.pallas import tpu as pltpu
from jax.sharding import PartitionSpec as P


HDIM = 64
GROUPS = 3
RING = 4
EPSILON = 1e-06
GUIDANCE = 6.0
F32 = jnp.float32
BF16 = jnp.bfloat16
VMEM = pltpu.VMEM
IN_VMEM = pl.BlockSpec(memory_space=VMEM)
IN_SMEM = pl.BlockSpec(memory_space=pltpu.SMEM)
IN_HBM = pl.BlockSpec(memory_space=pltpu.HBM)
LOOSE = pl.BlockSpec(memory_space=pl.ANY)


def near_core(*arrays):
    return [pltpu.with_memory_space_constraint(a, VMEM) for a in arrays]


def far_away(*arrays):
    return [pltpu.with_memory_space_constraint(a, pltpu.HBM) for a in arrays]


def cost(flops, moved, transcendentals=0):
    return pl.CostEstimate(flops=flops, bytes_accessed=moved, transcendentals=transcendentals)


def place():
    return lax.axis_index("tp"), lax.rem(lax.axis_index("queue"), 2)


def row_and_column():
    slot = lax.axis_index("queue")
    return lax.div(slot, 16), lax.rem(lax.div(slot, 2), 4)


def slice_kernel(w, out, sem):
    side, core = place()
    row, _ = row_and_column()
    depth, width = out.shape[1:]
    base = (1 - side) * (RING * width)
    source = pl.ds(pl.multiple_of(core * depth, depth), depth)
    copies = []
    for i in range(2):
        cols = pl.ds(pl.multiple_of(base + lax.rem(row + 2 * i, RING) * width, width), width)
        copies.append(pltpu.make_async_copy(w.at[source, cols], out.at[i], sem.at[i]))
        copies[-1].start()
    for copy in copies:
        copy.wait()


def local(kernel, outs, specs, flops, moved, *args, scratch=(), limit=1 << 20):
    placed = []
    for spec, arg in zip(specs, args):
        if spec is IN_VMEM:
            arg = near_core(arg)[0]
        elif spec is IN_HBM:
            arg = far_away(arg)[0]
        placed.append(arg)
    return pl.pallas_call(
        kernel,
        out_shape=outs,
        in_specs=list(specs),
        out_specs=jax.tree.map(lambda _: IN_VMEM, outs),
        scratch_shapes=list(scratch),
        cost_estimate=cost(flops, moved),
        compiler_params=pltpu.CompilerParams(vmem_limit_bytes=limit),
    )(*placed)


def prepare_kernel(
    step, keep, noise, level, text, w, mods, coefs, kept, row, words, ints, reals, sem, wsem
):
    first = pltpu.make_async_copy(step, ints, sem.at[0])
    small = [pltpu.make_async_copy(source, reals.at[i], sem.at[1 + i]) for i, source in enumerate((keep, noise))]
    small.append(pltpu.make_async_copy(text, words, sem.at[3]))
    first.start()
    for copy in small:
        copy.start()
    first.wait()
    at = ints[0]
    level_copy = pltpu.make_async_copy(level.at[pl.ds(at, 1)], row, sem.at[4])
    level_copy.start()
    weights = pltpu.make_async_copy(w, kept, wsem)
    weights.start()
    for copy in small:
        copy.wait()
    for i in range(2):
        coefs[i : i + 1, :] = jnp.full((1, coefs.shape[1]), reals[i, at], F32)
    level_copy.wait()
    for branch in range(2):
        mods[branch : branch + 1, :] = row[0, 0:1, :] + words[branch, 0:1, :]
        mods[2 + branch : 3 + branch, :] = 1.0 + (row[0, 1:2, :] + words[branch, 1:2, :])
    weights.wait()


def home_kernel(native, foreign, mods, coefs, w, out, normed, kept):
    half = foreign.shape[1]
    tokens = foreign.shape[0]
    side, _ = place()
    total = 2 * half
    parts = (native[0].astype(F32), foreign[...].astype(F32))
    mean = sum(jnp.sum(p, axis=-1, keepdims=True) for p in parts) / total
    parts = tuple(p - mean for p in parts)
    spread = sum(jnp.sum(p * p, axis=-1, keepdims=True) for p in parts) / total
    inverse = lax.rsqrt(spread + EPSILON)
    for part, where in zip(parts, (side, 1 - side)):
        unit = part * inverse
        cols = pl.ds(pl.multiple_of(where * half, half), half)
        for branch in range(2):
            shift = mods[branch : branch + 1, cols]
            gain = mods[2 + branch : 3 + branch, cols]
            normed[branch * tokens : (branch + 1) * tokens, cols] = (unit * gain + shift).astype(BF16)
    products(normed, w, 1, out, (1,))
    kept[...] = (coefs[0:1, 0:1] * native[0].astype(F32)).astype(BF16)


def products(normed, w, first, out, flip=()):
    width = out.shape[2] // GROUPS
    for i in range(out.shape[0]):
        for g in range(GROUPS):
            cols = slice(g * width, (g + 1) * width)
            value = jnp.dot(normed[...], w[first + i, :, cols], preferred_element_type=F32)
            out[i, :, cols] = (value.T if i in flip else value).astype(BF16)


def query_kernel(normed, w, w_out, back, ahead, out, columns, table, sem):
    side, _ = place()
    half = columns.shape[1]
    cols = pl.ds(pl.multiple_of(side * half, half), half)
    copy = pltpu.make_async_copy(w_out.at[:, cols], columns, sem)
    copy.start()
    count = lax.axis_size("queue")
    frame = lax.axis_index("queue")
    sense = 1 - 2 * lax.rem(frame, 2)
    for i, distance in enumerate((0, 1, -1, -2, 2)):
        offset = sense * distance
        target = frame + offset
        allowed = (offset >= -back[0]) & (offset <= ahead[0]) & (target >= 0) & (target < count)
        entry = jnp.where(allowed, 0.0, -1e30).astype(F32)
        table[i : i + 1, :] = jnp.full((1, table.shape[1]), entry, F32)
    products(normed, w, 0, out)
    copy.wait()


def scored(table, q, blocks, which, branch, g):
    width = q.shape[2] // GROUPS
    cols = slice(g * width, (g + 1) * width)
    tokens = q.shape[1] // 2
    at = slice(branch * tokens, (branch + 1) * tokens)
    flipped = slice(g * width + branch * tokens, g * width + (branch + 1) * tokens)
    heads = width // HDIM
    lane_head = lax.broadcasted_iota(jnp.int32, (1, width), 1) // HDIM
    keys = jnp.concatenate([block[0, at, cols] for block in blocks], axis=0)
    values = jnp.concatenate([block[1, :, flipped] for block in blocks], axis=1)
    query = q[0, at, cols] * jnp.asarray(HDIM ** (-0.5), BF16)
    stacked = jnp.concatenate(
        [jnp.where(lane_head == h, query, jnp.zeros_like(query)) for h in range(heads)], axis=0
    )
    scores = lax.dot_general(keys, stacked, (((1,), (1,)), ((), ())), preferred_element_type=F32)
    scores = jnp.concatenate(
        [scores[i * tokens : (i + 1) * tokens] + table[w : w + 1, :] for i, w in enumerate(which)], axis=0
    )
    return scores, values


def first_kernel(table, q, *refs):
    *blocks, sums, tops, totals = refs
    for g in range(GROUPS):
        for branch in range(2):
            scores, values = scored(table, q, blocks, (0, 1, 2, 4), branch, g)
            top = jnp.max(scores, axis=0, keepdims=True)
            expon = jnp.exp(scores - top)
            spot = 2 * g + branch
            sums[spot] = jnp.dot(values, expon.astype(BF16), preferred_element_type=F32)
            tops[spot : spot + 1, :] = top
            totals[spot : spot + 1, :] = jnp.sum(expon, axis=0, keepdims=True)


def second_kernel(table, coefs, q, block, sums, tops, totals, out):
    width = q.shape[2] // GROUPS
    tokens = q.shape[1] // 2
    noise = coefs[1:2, 0:1]
    for g in range(GROUPS):
        results = []
        for branch in range(2):
            spot = 2 * g + branch
            scores, values = scored(table, q, [block], (3,), branch, g)
            before = tops[spot : spot + 1, :]
            top = jnp.maximum(before, jnp.max(scores, axis=0, keepdims=True))
            expon = jnp.exp(scores - top)
            old = jnp.exp(before - top)
            scale = 1.0 / (old * totals[spot : spot + 1, :] + jnp.sum(expon, axis=0, keepdims=True))
            fresh = jnp.dot(values, expon.astype(BF16), preferred_element_type=F32)
            picked = []
            for h in range(width // HDIM):
                dims, lanes = slice(h * HDIM, (h + 1) * HDIM), slice(h * tokens, (h + 1) * tokens)
                mixed = old[:, lanes] * sums[spot, dims, lanes] + fresh[dims, lanes]
                picked.append((mixed * scale[:, lanes]).astype(BF16).astype(F32))
            results.append(jnp.concatenate(picked, axis=0))
        cond, plain = results
        out[:, g * width : (g + 1) * width] = (-noise * (plain + GUIDANCE * (cond - plain))).T.astype(BF16)


def final_kernel(before, mix, other, own, *refs):
    *pieces, out = refs
    _, core = place()
    row, column = row_and_column()
    block, part = pieces[0].shape[1:]
    low, high = other[:, :block], other[:, block:]
    mixed = jnp.concatenate([jnp.where(core == 0, low, high), jnp.where(core == 0, high, low)], axis=1)
    beside = jnp.where(column >= 2, RING - 1, 1)
    for i, turn in enumerate((0, 2, beside, beside + 2)):
        mine, mate = pieces[2 * (i // 2)], pieces[2 * (i // 2) + 1]
        cols = pl.ds(pl.multiple_of(lax.rem(row + turn, RING) * part, part), part)
        remote = jnp.concatenate([mine[i % 2], mate[i % 2]], axis=0)
        change = jnp.dot(mix[...], own[:, cols], preferred_element_type=F32)
        change = change + jnp.dot(mixed, remote, preferred_element_type=F32)
        out[0, :, cols] = (before[:, cols].astype(F32) + change).astype(BF16)


def body(
    latent,
    step_index,
    back_reach,
    ahead_reach,
    level_mod,
    text_mod,
    w_qkv,
    w_out,
    keep_coef,
    noise_coef,
):
    count = lax.axis_size("queue")
    every = range(count)
    onward = [(s, (s + 1) % count) for s in every]
    across = [(2 * s + t, 2 * ((s + 1) % count) + 1 - t) for s in every for t in range(2)]
    mates = [(s, s ^ 1) for s in every]
    near = [(s, s + 1 if s % 2 else s - 1) for s in every]
    far = [(s, s - 2 if s % 2 else s + 2) for s in every]
    near, far = ([(s, d) for s, d in pairs if 0 <= d < count] for pairs in (near, far))
    swap = [(0, 1), (1, 0)]
    tokens = latent.shape[1]
    half = latent.shape[2]

    def send(value, axis, pairs):
        return lax.ppermute(value, axis, pairs)

    width = w_qkv.shape[2]
    rows = 2 * tokens
    full = 2 * half
    heads = width // (GROUPS * HDIM)
    kv_shape = VMEM((2, rows, width), BF16)
    normed_shape = VMEM((rows, full), BF16)
    sems = lambda n: pltpu.SemaphoreType.DMA((n,))
    sem = pltpu.SemaphoreType.DMA
    work = 4 * rows * full * width

    ring = []
    for slot in every:
        step = 16 if (slot // 2) % 4 >= 2 else -16
        ring.append((slot, (slot + step) % count))
    mirror = [(2 * slot + t, 2 * (slot ^ 8) + 1 - t) for slot in every for t in range(2)]
    foreign = send(latent[0], "tp", swap)
    mods, coefs, weights = local(
        prepare_kernel,
        (
            VMEM((4, full), F32), VMEM((8, 128), F32), VMEM(w_qkv.shape, BF16),
        ),
        (LOOSE,) + (IN_HBM,) * 5, 0, 4 * w_qkv.size,
        step_index, keep_coef, noise_coef, level_mod, text_mod, w_qkv,
        scratch=(
            VMEM((1, 2, full), F32), VMEM((2, 2, full), F32), pltpu.SMEM((1,), jnp.int32),
            pltpu.SMEM((2, keep_coef.shape[0]), F32), sems(5), sem,
        ),
    )
    sliced = local(
        slice_kernel, VMEM((2, width // 2, half // RING), BF16), (IN_HBM,), 0, 2 * w_out.size, w_out,
        scratch=(sems(2),),
    )
    across_rows = send(sliced, ("queue", "tp"), mirror)
    beside_rows = send(across_rows, "queue", ring)
    remote = (across_rows, send(across_rows, "queue", mates), beside_rows, send(beside_rows, "queue", mates))
    kv, normed, scaled = local(
        home_kernel, (kv_shape, normed_shape, VMEM((tokens, half), BF16)), (IN_VMEM,) * 5, work, 4 * w_qkv.size,
        latent, foreign, mods, coefs, weights, limit=12 << 20,
    )
    before = send(scaled, "queue", onward)
    near_kv = send(kv, "queue", near)
    mate_kv = send(kv, "queue", mates)
    far_kv = send(mate_kv, "queue", near)
    passed_kv = send(near_kv, "queue", mates)
    q, w_columns, table = local(
        query_kernel, (VMEM((1, rows, width), BF16), VMEM((width, half), BF16), VMEM((8, heads * tokens), F32)),
        (IN_VMEM, IN_VMEM, IN_HBM, IN_SMEM, IN_SMEM), work // 2, 2 * w_qkv.size, normed, weights, w_out,
        back_reach, ahead_reach, scratch=(sem,), limit=12 << 20,
    )
    pairs = 2 * GROUPS
    sums, tops, totals = local(
        first_kernel,
        (
            VMEM((pairs, width // GROUPS, heads * tokens), F32), VMEM((8, heads * tokens), F32),
            VMEM((8, heads * tokens), F32),
        ),
        (IN_VMEM,) * 6, work, 32 * rows * width, table, q, kv, mate_kv, near_kv, passed_kv, limit=12 << 20,
    )
    mix = local(
        second_kernel, VMEM((tokens, width), BF16), (IN_VMEM,) * 7, work // 4, 32 * rows * width,
        table, coefs, q, far_kv, sums, tops, totals, limit=12 << 20,
    )

    mix_there = send(mix, ("queue", "tp"), across)
    mix_here = send(mix, "queue", onward)
    return pl.pallas_call(
        final_kernel,
        out_shape=jax.ShapeDtypeStruct((1, tokens, half), BF16),
        in_specs=[IN_VMEM] * 8,
        out_specs=IN_VMEM,
        cost_estimate=cost(4 * tokens * width * half, 8 * width * half),
        compiler_params=pltpu.CompilerParams(vmem_limit_bytes=12 << 20),
        name="final",
    )(*near_core(before, mix_here, mix_there, w_columns, *remote))


def solution(mesh):
    return jax.shard_map(
        body,
        mesh=mesh,
        in_specs=(
            P("queue", None, "tp"),
            P("queue"),
            P("queue"),
            P("queue"),
            P(),
            P(),
            P(None, None, "tp"),
            P("tp", None),
            P(),
            P(),
        ),
        out_specs=P("queue", None, "tp"),
        check_vma=False,
    )
```

```python
import jax
import jax.numpy as jnp
from jax import lax
from jax.experimental import pallas as pl
from jax.experimental.pallas import tpu as pltpu
from jax.sharding import PartitionSpec as P


HDIM = 64
GROUPS = 3
RING = 4
EPSILON = 1e-06
GUIDANCE = 6.0
F32 = jnp.float32
BF16 = jnp.bfloat16
VMEM = pltpu.VMEM
IN_VMEM = pl.BlockSpec(memory_space=VMEM)
IN_SMEM = pl.BlockSpec(memory_space=pltpu.SMEM)
IN_HBM = pl.BlockSpec(memory_space=pltpu.HBM)
LOOSE = pl.BlockSpec(memory_space=pl.ANY)


def near_core(*arrays):
    return [pltpu.with_memory_space_constraint(a, VMEM) for a in arrays]


def far_away(*arrays):
    return [pltpu.with_memory_space_constraint(a, pltpu.HBM) for a in arrays]


def cost(flops, moved, transcendentals=0):
    return pl.CostEstimate(flops=flops, bytes_accessed=moved, transcendentals=transcendentals)


def place():
    return lax.axis_index("tp"), lax.rem(lax.axis_index("queue"), 2)


def row_and_column():
    slot = lax.axis_index("queue")
    return lax.div(slot, 16), lax.rem(lax.div(slot, 2), 4)


def slice_kernel(w, out, sem):
    side, core = place()
    row, _ = row_and_column()
    depth, width = out.shape[1:]
    base = (1 - side) * (RING * width)
    source = pl.ds(pl.multiple_of(core * depth, depth), depth)
    copies = []
    for i in range(2):
        cols = pl.ds(pl.multiple_of(base + lax.rem(row + 2 * i, RING) * width, width), width)
        copies.append(pltpu.make_async_copy(w.at[source, cols], out.at[i], sem.at[i]))
        copies[-1].start()
    for copy in copies:
        copy.wait()


def local(kernel, outs, specs, flops, moved, *args, scratch=(), limit=1 << 20):
    placed = []
    for spec, arg in zip(specs, args):
        if spec is IN_VMEM:
            arg = near_core(arg)[0]
        elif spec is IN_HBM:
            arg = far_away(arg)[0]
        placed.append(arg)
    return pl.pallas_call(
        kernel,
        out_shape=outs,
        in_specs=list(specs),
        out_specs=jax.tree.map(lambda _: IN_VMEM, outs),
        scratch_shapes=list(scratch),
        cost_estimate=cost(flops, moved),
        compiler_params=pltpu.CompilerParams(vmem_limit_bytes=limit),
    )(*placed)


def prepare_kernel(
    step, keep, noise, level, text, w, mods, coefs, kept, row, words, ints, reals, sem, wsem
):
    first = pltpu.make_async_copy(step, ints, sem.at[0])
    small = [pltpu.make_async_copy(source, reals.at[i], sem.at[1 + i]) for i, source in enumerate((keep, noise))]
    small.append(pltpu.make_async_copy(text, words, sem.at[3]))
    first.start()
    for copy in small:
        copy.start()
    first.wait()
    at = ints[0]
    level_copy = pltpu.make_async_copy(level.at[pl.ds(at, 1)], row, sem.at[4])
    level_copy.start()
    weights = pltpu.make_async_copy(w.at[pl.ds(1, 2)], kept, wsem)
    weights.start()
    for copy in small:
        copy.wait()
    for i in range(2):
        coefs[i : i + 1, :] = jnp.full((1, coefs.shape[1]), reals[i, at], F32)
    level_copy.wait()
    for branch in range(2):
        mods[branch : branch + 1, :] = row[0, 0:1, :] + words[branch, 0:1, :]
        mods[2 + branch : 3 + branch, :] = 1.0 + (row[0, 1:2, :] + words[branch, 1:2, :])
    weights.wait()


def home_kernel(native, foreign, mods, coefs, w, out, normed, kept):
    half = foreign.shape[1]
    tokens = foreign.shape[0]
    side, _ = place()
    total = 2 * half
    parts = (native[0].astype(F32), foreign[...].astype(F32))
    mean = sum(jnp.sum(p, axis=-1, keepdims=True) for p in parts) / total
    parts = tuple(p - mean for p in parts)
    spread = sum(jnp.sum(p * p, axis=-1, keepdims=True) for p in parts) / total
    inverse = lax.rsqrt(spread + EPSILON)
    for part, where in zip(parts, (side, 1 - side)):
        unit = part * inverse
        cols = pl.ds(pl.multiple_of(where * half, half), half)
        for branch in range(2):
            shift = mods[branch : branch + 1, cols]
            gain = mods[2 + branch : 3 + branch, cols]
            normed[branch * tokens : (branch + 1) * tokens, cols] = (unit * gain + shift).astype(BF16)
    products(normed, w, 0, out, (1,))
    kept[...] = (coefs[0:1, 0:1] * native[0].astype(F32)).astype(BF16)


def products(normed, w, first, out, flip=()):
    width = out.shape[2] // GROUPS
    for i in range(out.shape[0]):
        for g in range(GROUPS):
            cols = slice(g * width, (g + 1) * width)
            value = jnp.dot(normed[...], w[first + i, :, cols], preferred_element_type=F32)
            out[i, :, cols] = (value.T if i in flip else value).astype(BF16)


def query_kernel(normed, w, w_out, back, ahead, out, columns, table, kept, sem, wsem):
    side, _ = place()
    half = columns.shape[1]
    cols = pl.ds(pl.multiple_of(side * half, half), half)
    weights = pltpu.make_async_copy(w.at[pl.ds(0, 1)], kept, wsem)
    weights.start()
    copy = pltpu.make_async_copy(w_out.at[:, cols], columns, sem)
    copy.start()
    count = lax.axis_size("queue")
    frame = lax.axis_index("queue")
    sense = 1 - 2 * lax.rem(frame, 2)
    for i, distance in enumerate((0, 1, -1, -2, 2)):
        offset = sense * distance
        target = frame + offset
        allowed = (offset >= -back[0]) & (offset <= ahead[0]) & (target >= 0) & (target < count)
        entry = jnp.where(allowed, 0.0, -1e30).astype(F32)
        table[i : i + 1, :] = jnp.full((1, table.shape[1]), entry, F32)
    weights.wait()
    products(normed, kept, 0, out)
    copy.wait()


def scored(table, q, blocks, which, branch, g):
    width = q.shape[2] // GROUPS
    cols = slice(g * width, (g + 1) * width)
    tokens = q.shape[1] // 2
    at = slice(branch * tokens, (branch + 1) * tokens)
    flipped = slice(g * width + branch * tokens, g * width + (branch + 1) * tokens)
    heads = width // HDIM
    lane_head = lax.broadcasted_iota(jnp.int32, (1, width), 1) // HDIM
    keys = jnp.concatenate([block[0, at, cols] for block in blocks], axis=0)
    values = jnp.concatenate([block[1, :, flipped] for block in blocks], axis=1)
    query = q[0, at, cols] * jnp.asarray(HDIM ** (-0.5), BF16)
    stacked = jnp.concatenate(
        [jnp.where(lane_head == h, query, jnp.zeros_like(query)) for h in range(heads)], axis=0
    )
    scores = lax.dot_general(keys, stacked, (((1,), (1,)), ((), ())), preferred_element_type=F32)
    scores = jnp.concatenate(
        [scores[i * tokens : (i + 1) * tokens] + table[w : w + 1, :] for i, w in enumerate(which)], axis=0
    )
    return scores, values


def first_kernel(table, q, *refs):
    *blocks, sums, tops, totals = refs
    for g in range(GROUPS):
        for branch in range(2):
            scores, values = scored(table, q, blocks, (0, 1, 2, 4), branch, g)
            top = jnp.max(scores, axis=0, keepdims=True)
            expon = jnp.exp(scores - top)
            spot = 2 * g + branch
            sums[spot] = jnp.dot(values, expon.astype(BF16), preferred_element_type=F32)
            tops[spot : spot + 1, :] = top
            totals[spot : spot + 1, :] = jnp.sum(expon, axis=0, keepdims=True)


def second_kernel(table, coefs, q, block, sums, tops, totals, out):
    width = q.shape[2] // GROUPS
    tokens = q.shape[1] // 2
    noise = coefs[1:2, 0:1]
    for g in range(GROUPS):
        results = []
        for branch in range(2):
            spot = 2 * g + branch
            scores, values = scored(table, q, [block], (3,), branch, g)
            before = tops[spot : spot + 1, :]
            top = jnp.maximum(before, jnp.max(scores, axis=0, keepdims=True))
            expon = jnp.exp(scores - top)
            old = jnp.exp(before - top)
            scale = 1.0 / (old * totals[spot : spot + 1, :] + jnp.sum(expon, axis=0, keepdims=True))
            fresh = jnp.dot(values, expon.astype(BF16), preferred_element_type=F32)
            picked = []
            for h in range(width // HDIM):
                dims, lanes = slice(h * HDIM, (h + 1) * HDIM), slice(h * tokens, (h + 1) * tokens)
                mixed = old[:, lanes] * sums[spot, dims, lanes] + fresh[dims, lanes]
                picked.append((mixed * scale[:, lanes]).astype(BF16).astype(F32))
            results.append(jnp.concatenate(picked, axis=0))
        cond, plain = results
        out[:, g * width : (g + 1) * width] = (-noise * (plain + GUIDANCE * (cond - plain))).T.astype(BF16)


def early_kernel(before, other, *refs):
    *pieces, out = refs
    _, core = place()
    row, column = row_and_column()
    block, part = pieces[0].shape[1:]
    low, high = other[:, :block], other[:, block:]
    halves = (jnp.where(core == 0, low, high), jnp.where(core == 0, high, low))
    beside = jnp.where(column >= 2, RING - 1, 1)
    for i, turn in enumerate((0, 2, beside, beside + 2)):
        cols = pl.ds(pl.multiple_of(lax.rem(row + turn, RING) * part, part), part)
        total = before[:, cols].astype(F32)
        for half, piece in zip(halves, pieces[2 * (i // 2) : 2 * (i // 2) + 2]):
            total = total + jnp.dot(half, piece[i % 2], preferred_element_type=F32)
        out[:, cols] = total


def final_kernel(early, mix, own, out):
    step = 512
    for i in range(own.shape[1] // step):
        cols = slice(i * step, (i + 1) * step)
        out[0, :, cols] = (early[:, cols] + jnp.dot(mix[...], own[:, cols], preferred_element_type=F32)).astype(BF16)


def body(
    latent,
    step_index,
    back_reach,
    ahead_reach,
    level_mod,
    text_mod,
    w_qkv,
    w_out,
    keep_coef,
    noise_coef,
):
    count = lax.axis_size("queue")
    every = range(count)
    onward = [(s, (s + 1) % count) for s in every]
    across = [(2 * s + t, 2 * ((s + 1) % count) + 1 - t) for s in every for t in range(2)]
    mates = [(s, s ^ 1) for s in every]
    near = [(s, s + 1 if s % 2 else s - 1) for s in every]
    far = [(s, s - 2 if s % 2 else s + 2) for s in every]
    near, far = ([(s, d) for s, d in pairs if 0 <= d < count] for pairs in (near, far))
    swap = [(0, 1), (1, 0)]
    tokens = latent.shape[1]
    half = latent.shape[2]

    def send(value, axis, pairs):
        return lax.ppermute(value, axis, pairs)

    width = w_qkv.shape[2]
    rows = 2 * tokens
    full = 2 * half
    heads = width // (GROUPS * HDIM)
    kv_shape = VMEM((2, rows, width), BF16)
    normed_shape = VMEM((rows, full), BF16)
    sems = lambda n: pltpu.SemaphoreType.DMA((n,))
    sem = pltpu.SemaphoreType.DMA
    work = 4 * rows * full * width

    ring = []
    for slot in every:
        step = 16 if (slot // 2) % 4 >= 2 else -16
        ring.append((slot, (slot + step) % count))
    mirror = [(2 * slot + t, 2 * (slot ^ 8) + 1 - t) for slot in every for t in range(2)]
    foreign = send(latent[0], "tp", swap)
    mods, coefs, weights = local(
        prepare_kernel,
        (
            VMEM((4, full), F32), VMEM((8, 128), F32), VMEM((2,) + w_qkv.shape[1:], BF16),
        ),
        (LOOSE,) + (IN_HBM,) * 5, 0, 4 * w_qkv.size,
        step_index, keep_coef, noise_coef, level_mod, text_mod, w_qkv,
        scratch=(
            VMEM((1, 2, full), F32), VMEM((2, 2, full), F32), pltpu.SMEM((1,), jnp.int32),
            pltpu.SMEM((2, keep_coef.shape[0]), F32), sems(5), sem,
        ),
    )
    sliced = local(
        slice_kernel, VMEM((2, width // 2, half // RING), BF16), (IN_HBM,), 0, 2 * w_out.size, w_out,
        scratch=(sems(2),),
    )
    across_rows = send(sliced, ("queue", "tp"), mirror)
    beside_rows = send(across_rows, "queue", ring)
    remote = (across_rows, send(across_rows, "queue", mates), beside_rows, send(beside_rows, "queue", mates))
    kv, normed, scaled = local(
        home_kernel, (kv_shape, normed_shape, VMEM((tokens, half), BF16)), (IN_VMEM,) * 5, work, 4 * w_qkv.size,
        latent, foreign, mods, coefs, weights, limit=12 << 20,
    )
    before = send(scaled, "queue", onward)
    near_kv = send(kv, "queue", near)
    mate_kv = send(kv, "queue", mates)
    far_kv = send(mate_kv, "queue", near)
    passed_kv = send(near_kv, "queue", mates)
    q, w_columns, table = local(
        query_kernel, (VMEM((1, rows, width), BF16), VMEM((width, half), BF16), VMEM((8, heads * tokens), F32)),
        (IN_VMEM, IN_HBM, IN_HBM, IN_SMEM, IN_SMEM), work // 2, 2 * w_qkv.size, normed, w_qkv, w_out,
        back_reach, ahead_reach, scratch=(VMEM((1,) + w_qkv.shape[1:], BF16), sem, sem), limit=16 << 20,
    )
    pairs = 2 * GROUPS
    sums, tops, totals = local(
        first_kernel,
        (
            VMEM((pairs, width // GROUPS, heads * tokens), F32), VMEM((8, heads * tokens), F32),
            VMEM((8, heads * tokens), F32),
        ),
        (IN_VMEM,) * 6, work, 32 * rows * width, table, q, kv, mate_kv, near_kv, passed_kv, limit=12 << 20,
    )
    mix = local(
        second_kernel, VMEM((tokens, width), BF16), (IN_VMEM,) * 7, work // 4, 32 * rows * width,
        table, coefs, q, far_kv, sums, tops, totals, limit=12 << 20,
    )

    mix_there = send(mix, ("queue", "tp"), across)
    mix_here = send(mix, "queue", onward)
    early = local(
        early_kernel, VMEM((tokens, half), F32), (IN_VMEM,) * 6, 2 * tokens * width * half, 4 * width * half,
        before, mix_there, *remote, limit=8 << 20,
    )
    return pl.pallas_call(
        final_kernel,
        out_shape=jax.ShapeDtypeStruct((1, tokens, half), BF16),
        in_specs=[IN_VMEM] * 3,
        out_specs=IN_VMEM,
        cost_estimate=cost(2 * tokens * width * half, 4 * width * half),
        compiler_params=pltpu.CompilerParams(vmem_limit_bytes=8 << 20),
        name="final",
    )(*near_core(early, mix_here, w_columns))


def solution(mesh):
    return jax.shard_map(
        body,
        mesh=mesh,
        in_specs=(
            P("queue", None, "tp"),
            P("queue"),
            P("queue"),
            P("queue"),
            P(),
            P(),
            P(None, None, "tp"),
            P("tp", None),
            P(),
            P(),
        ),
        out_specs=P("queue", None, "tp"),
        check_vma=False,
    )
```

```python
import jax
import jax.numpy as jnp
from jax import lax
from jax.experimental import pallas as pl
from jax.experimental.pallas import tpu as pltpu
from jax.sharding import PartitionSpec as P


HDIM = 64
GROUPS = 3
RING = 4
BUSY = 10**10
EPSILON = 1e-06
GUIDANCE = 6.0
F32 = jnp.float32
BF16 = jnp.bfloat16
VMEM = pltpu.VMEM
IN_VMEM = pl.BlockSpec(memory_space=VMEM)
IN_SMEM = pl.BlockSpec(memory_space=pltpu.SMEM)
IN_HBM = pl.BlockSpec(memory_space=pltpu.HBM)
LOOSE = pl.BlockSpec(memory_space=pl.ANY)


def near_core(*arrays):
    return [pltpu.with_memory_space_constraint(a, VMEM) for a in arrays]


def far_away(*arrays):
    return [pltpu.with_memory_space_constraint(a, pltpu.HBM) for a in arrays]


def cost(flops, moved, transcendentals=0):
    return pl.CostEstimate(flops=flops, bytes_accessed=moved, transcendentals=transcendentals)


def place():
    return lax.axis_index("tp"), lax.rem(lax.axis_index("queue"), 2)


def row_and_column():
    slot = lax.axis_index("queue")
    return lax.div(slot, 16), lax.rem(lax.div(slot, 2), 4)


def slice_kernel(w, out, sem):
    side, core = place()
    row, _ = row_and_column()
    depth, width = out.shape[1:]
    base = (1 - side) * (RING * width)
    source = pl.ds(pl.multiple_of(core * depth, depth), depth)
    copies = []
    for i in range(2):
        cols = pl.ds(pl.multiple_of(base + lax.rem(row + 2 * i, RING) * width, width), width)
        copies.append(pltpu.make_async_copy(w.at[source, cols], out.at[i], sem.at[i]))
        copies[-1].start()
    for copy in copies:
        copy.wait()


def local(kernel, outs, specs, flops, moved, *args, scratch=(), limit=1 << 20):
    placed = []
    for spec, arg in zip(specs, args):
        if spec is IN_VMEM:
            arg = near_core(arg)[0]
        elif spec is IN_HBM:
            arg = far_away(arg)[0]
        placed.append(arg)
    return pl.pallas_call(
        kernel,
        out_shape=outs,
        in_specs=list(specs),
        out_specs=jax.tree.map(lambda _: IN_VMEM, outs),
        scratch_shapes=list(scratch),
        cost_estimate=cost(flops, moved),
        compiler_params=pltpu.CompilerParams(vmem_limit_bytes=limit),
    )(*placed)


def prepare_kernel(
    step, keep, noise, level, text, mods, coefs, row, words, ints, reals, sem
):
    first = pltpu.make_async_copy(step, ints, sem.at[0])
    small = [pltpu.make_async_copy(source, reals.at[i], sem.at[1 + i]) for i, source in enumerate((keep, noise))]
    small.append(pltpu.make_async_copy(text, words, sem.at[3]))
    first.start()
    for copy in small:
        copy.start()
    first.wait()
    at = ints[0]
    level_copy = pltpu.make_async_copy(level.at[pl.ds(at, 1)], row, sem.at[4])
    level_copy.start()
    for copy in small:
        copy.wait()
    for i in range(2):
        coefs[i : i + 1, :] = jnp.full((1, coefs.shape[1]), reals[i, at], F32)
    level_copy.wait()
    for branch in range(2):
        mods[branch : branch + 1, :] = row[0, 0:1, :] + words[branch, 0:1, :]
        mods[2 + branch : 3 + branch, :] = 1.0 + (row[0, 1:2, :] + words[branch, 1:2, :])


def home_kernel(native, foreign, mods, coefs, w, out, normed, kept):
    half = foreign.shape[1]
    tokens = foreign.shape[0]
    side, _ = place()
    total = 2 * half
    parts = (native[0].astype(F32), foreign[...].astype(F32))
    mean = sum(jnp.sum(p, axis=-1, keepdims=True) for p in parts) / total
    parts = tuple(p - mean for p in parts)
    spread = sum(jnp.sum(p * p, axis=-1, keepdims=True) for p in parts) / total
    inverse = lax.rsqrt(spread + EPSILON)
    for part, where in zip(parts, (side, 1 - side)):
        unit = part * inverse
        cols = pl.ds(pl.multiple_of(where * half, half), half)
        for branch in range(2):
            shift = mods[branch : branch + 1, cols]
            gain = mods[2 + branch : 3 + branch, cols]
            normed[branch * tokens : (branch + 1) * tokens, cols] = (unit * gain + shift).astype(BF16)
    products(normed, w, 1, out, (1,))
    kept[...] = (coefs[0:1, 0:1] * native[0].astype(F32)).astype(BF16)


def products(normed, w, first, out, flip=()):
    width = out.shape[2] // GROUPS
    for i in range(out.shape[0]):
        for g in range(GROUPS):
            cols = slice(g * width, (g + 1) * width)
            value = jnp.dot(normed[...], w[first + i, :, cols], preferred_element_type=F32)
            out[i, :, cols] = (value.T if i in flip else value).astype(BF16)


def query_kernel(normed, w, w_out, back, ahead, out, columns, table, sem):
    side, _ = place()
    half = columns.shape[1]
    cols = pl.ds(pl.multiple_of(side * half, half), half)
    copy = pltpu.make_async_copy(w_out.at[:, cols], columns, sem)
    copy.start()
    count = lax.axis_size("queue")
    frame = lax.axis_index("queue")
    sense = 1 - 2 * lax.rem(frame, 2)
    for i, distance in enumerate((0, 1, -1, -2, 2)):
        offset = sense * distance
        target = frame + offset
        allowed = (offset >= -back[0]) & (offset <= ahead[0]) & (target >= 0) & (target < count)
        entry = jnp.where(allowed, 0.0, -1e30).astype(F32)
        table[i : i + 1, :] = jnp.full((1, table.shape[1]), entry, F32)
    products(normed, w, 0, out)
    copy.wait()


def scored(table, q, keys, which, branch, g):
    width = q.shape[2] // GROUPS
    cols = slice(g * width, (g + 1) * width)
    tokens = q.shape[1] // 2
    at = slice(branch * tokens, (branch + 1) * tokens)
    heads = width // HDIM
    lane_head = lax.broadcasted_iota(jnp.int32, (1, width), 1) // HDIM
    keys = jnp.concatenate([key[at, cols] for key in keys], axis=0)
    query = q[0, at, cols] * jnp.asarray(HDIM ** (-0.5), BF16)
    stacked = jnp.concatenate(
        [jnp.where(lane_head == h, query, jnp.zeros_like(query)) for h in range(heads)], axis=0
    )
    scores = lax.dot_general(keys, stacked, (((1,), (1,)), ((), ())), preferred_element_type=F32)
    return jnp.concatenate(
        [scores[i * tokens : (i + 1) * tokens] + table[w : w + 1, :] for i, w in enumerate(which)], axis=0
    )


def flipped(tokens, width, branch, g):
    return slice(g * width + branch * tokens, g * width + (branch + 1) * tokens)


def first_kernel(table, q, own, mate, close, passed, sums, tops, totals):
    tokens = q.shape[1] // 2
    width = q.shape[2] // GROUPS
    for g in range(GROUPS):
        for branch in range(2):
            scores = scored(table, q, [block.at[0] for block in (own, mate, close, passed)], (0, 1, 2, 4), branch, g)
            at = flipped(tokens, width, branch, g)
            values = jnp.concatenate([block[1, :, at] for block in (own, mate, close, passed)], axis=1)
            top = jnp.max(scores, axis=0, keepdims=True)
            expon = jnp.exp(scores - top)
            spot = 2 * g + branch
            sums[spot] = jnp.dot(values, expon.astype(BF16), preferred_element_type=F32)
            tops[spot : spot + 1, :] = top
            totals[spot : spot + 1, :] = jnp.sum(expon, axis=0, keepdims=True)


def second_kernel(table, q, far, tops, totals, weights, scales):
    for g in range(GROUPS):
        for branch in range(2):
            spot = 2 * g + branch
            scores = scored(table, q, [far.at[0]], (3,), branch, g)
            before = tops[spot : spot + 1, :]
            top = jnp.maximum(before, jnp.max(scores, axis=0, keepdims=True))
            expon = jnp.exp(scores - top)
            old = jnp.exp(before - top)
            scale = 1.0 / (old * totals[spot : spot + 1, :] + jnp.sum(expon, axis=0, keepdims=True))
            weights[spot] = expon.astype(BF16)
            scales[spot : spot + 1, :] = scale
            scales[8 + spot : 9 + spot, :] = old * scale


def third_kernel(coefs, far, weights, scales, sums, out):
    width = out.shape[1] // GROUPS
    tokens = out.shape[0]
    noise = coefs[1:2, 0:1]
    for g in range(GROUPS):
        results = []
        for branch in range(2):
            spot = 2 * g + branch
            values = far[1, :, flipped(tokens, width, branch, g)]
            fresh = jnp.dot(values, weights[spot], preferred_element_type=F32)
            picked = []
            for h in range(width // HDIM):
                dims, lanes = slice(h * HDIM, (h + 1) * HDIM), slice(h * tokens, (h + 1) * tokens)
                mixed = scales[8 + spot : 9 + spot, lanes] * sums[spot, dims, lanes]
                mixed = mixed + scales[spot : spot + 1, lanes] * fresh[dims, lanes]
                picked.append(mixed.astype(BF16).astype(F32))
            results.append(jnp.concatenate(picked, axis=0))
        cond, plain = results
        out[:, g * width : (g + 1) * width] = (-noise * (plain + GUIDANCE * (cond - plain))).T.astype(BF16)


def early_kernel(before, other, *refs):
    *pieces, out = refs
    _, core = place()
    row, column = row_and_column()
    block, part = pieces[0].shape[1:]
    low, high = other[:, :block], other[:, block:]
    halves = (jnp.where(core == 0, low, high), jnp.where(core == 0, high, low))
    beside = jnp.where(column >= 2, RING - 1, 1)
    for i, turn in enumerate((0, 2, beside, beside + 2)):
        cols = pl.ds(pl.multiple_of(lax.rem(row + turn, RING) * part, part), part)
        total = before[:, cols].astype(F32)
        for half, piece in zip(halves, pieces[2 * (i // 2) : 2 * (i // 2) + 2]):
            total = total + jnp.dot(half, piece[i % 2], preferred_element_type=F32)
        out[:, cols] = total


def final_kernel(early, mix, own, out):
    step = 512
    for i in range(own.shape[1] // step):
        cols = slice(i * step, (i + 1) * step)
        out[0, :, cols] = (early[:, cols] + jnp.dot(mix[...], own[:, cols], preferred_element_type=F32)).astype(BF16)


def body(
    latent,
    step_index,
    back_reach,
    ahead_reach,
    level_mod,
    text_mod,
    w_qkv,
    w_out,
    keep_coef,
    noise_coef,
):
    count = lax.axis_size("queue")
    every = range(count)
    onward = [(s, (s + 1) % count) for s in every]
    across = [(2 * s + t, 2 * ((s + 1) % count) + 1 - t) for s in every for t in range(2)]
    mates = [(s, s ^ 1) for s in every]
    near = [(s, s + 1 if s % 2 else s - 1) for s in every]
    far = [(s, s - 2 if s % 2 else s + 2) for s in every]
    near, far = ([(s, d) for s, d in pairs if 0 <= d < count] for pairs in (near, far))
    swap = [(0, 1), (1, 0)]
    tokens = latent.shape[1]
    half = latent.shape[2]

    def send(value, axis, pairs):
        return lax.ppermute(value, axis, pairs)

    width = w_qkv.shape[2]
    rows = 2 * tokens
    full = 2 * half
    heads = width // (GROUPS * HDIM)
    kv_shape = VMEM((2, rows, width), BF16)
    normed_shape = VMEM((rows, full), BF16)
    sems = lambda n: pltpu.SemaphoreType.DMA((n,))
    sem = pltpu.SemaphoreType.DMA
    work = 4 * rows * full * width

    ring = []
    for slot in every:
        step = 16 if (slot // 2) % 4 >= 2 else -16
        ring.append((slot, (slot + step) % count))
    mirror = [(2 * slot + t, 2 * (slot ^ 8) + 1 - t) for slot in every for t in range(2)]
    foreign = send(latent[0], "tp", swap)
    mods, coefs = local(
        prepare_kernel,
        (
            VMEM((4, full), F32), VMEM((8, 128), F32),
        ),
        (LOOSE,) + (IN_HBM,) * 4, BUSY, 4 * w_qkv.size,
        step_index, keep_coef, noise_coef, level_mod, text_mod,
        scratch=(
            VMEM((1, 2, full), F32), VMEM((2, 2, full), F32), pltpu.SMEM((1,), jnp.int32),
            pltpu.SMEM((2, keep_coef.shape[0]), F32), sems(5),
        ),
    )
    sliced = local(
        slice_kernel, VMEM((2, width // 2, half // RING), BF16), (IN_HBM,), BUSY, 2 * w_out.size, w_out,
        scratch=(sems(2),),
    )
    across_rows = send(sliced, ("queue", "tp"), mirror)
    beside_rows = send(across_rows, "queue", ring)
    remote = (across_rows, send(across_rows, "queue", mates), beside_rows, send(beside_rows, "queue", mates))
    kv, normed, scaled = local(
        home_kernel, (kv_shape, normed_shape, VMEM((tokens, half), BF16)), (IN_VMEM,) * 5, work, 4 * w_qkv.size,
        latent, foreign, mods, coefs, w_qkv, limit=12 << 20,
    )
    before = send(scaled, "queue", onward)
    near_kv = send(kv, "queue", near)
    mate_kv = send(kv, "queue", mates)
    far_kv = send(mate_kv, "queue", near)
    passed_kv = send(near_kv, "queue", mates)
    q, w_columns, table = local(
        query_kernel, (VMEM((1, rows, width), BF16), VMEM((width, half), BF16), VMEM((8, heads * tokens), F32)),
        (IN_VMEM, IN_VMEM, IN_HBM, IN_SMEM, IN_SMEM), work // 2, 2 * w_qkv.size, normed, w_qkv, w_out,
        back_reach, ahead_reach, scratch=(sem,), limit=12 << 20,
    )
    pairs = 2 * GROUPS
    sums, tops, totals = local(
        first_kernel,
        (
            VMEM((pairs, width // GROUPS, heads * tokens), F32), VMEM((8, heads * tokens), F32),
            VMEM((8, heads * tokens), F32),
        ),
        (IN_VMEM,) * 6, work, 32 * rows * width, table, q, kv, mate_kv, near_kv, passed_kv, limit=12 << 20,
    )
    chances, scales = local(
        second_kernel, (VMEM((pairs, tokens, heads * tokens), BF16), VMEM((16, heads * tokens), F32)),
        (IN_VMEM,) * 5, work // 8, 16 * rows * width, table, q, far_kv, tops, totals, limit=12 << 20,
    )
    mix = local(
        third_kernel, VMEM((tokens, width), BF16), (IN_VMEM,) * 5, work // 8, 16 * rows * width,
        coefs, far_kv, chances, scales, sums, limit=12 << 20,
    )
    mix_there = send(mix, ("queue", "tp"), across)
    mix_here = send(mix, "queue", onward)
    early = local(
        early_kernel, VMEM((tokens, half), F32), (IN_VMEM,) * 6, 2 * tokens * width * half, 4 * width * half,
        before, mix_there, *remote, limit=8 << 20,
    )
    return pl.pallas_call(
        final_kernel,
        out_shape=jax.ShapeDtypeStruct((1, tokens, half), BF16),
        in_specs=[IN_VMEM] * 3,
        out_specs=IN_VMEM,
        cost_estimate=cost(2 * tokens * width * half, 4 * width * half),
        compiler_params=pltpu.CompilerParams(vmem_limit_bytes=8 << 20),
        name="final",
    )(*near_core(early, mix_here, w_columns))


def solution(mesh):
    return jax.shard_map(
        body,
        mesh=mesh,
        in_specs=(
            P("queue", None, "tp"),
            P("queue"),
            P("queue"),
            P("queue"),
            P(),
            P(),
            P(None, None, "tp"),
            P("tp", None),
            P(),
            P(),
        ),
        out_specs=P("queue", None, "tp"),
        check_vma=False,
    )
```

```python
import jax
import jax.numpy as jnp
from jax import lax
from jax.experimental import pallas as pl
from jax.experimental.pallas import tpu as pltpu
from jax.sharding import PartitionSpec as P


HDIM = 64
GROUPS = 3
RING = 4
BUSY = 10**10
EPSILON = 1e-06
GUIDANCE = 6.0
F32 = jnp.float32
BF16 = jnp.bfloat16
VMEM = pltpu.VMEM
IN_VMEM = pl.BlockSpec(memory_space=VMEM)
IN_SMEM = pl.BlockSpec(memory_space=pltpu.SMEM)
IN_HBM = pl.BlockSpec(memory_space=pltpu.HBM)
LOOSE = pl.BlockSpec(memory_space=pl.ANY)


def near_core(*arrays):
    return [pltpu.with_memory_space_constraint(a, VMEM) for a in arrays]


def far_away(*arrays):
    return [pltpu.with_memory_space_constraint(a, pltpu.HBM) for a in arrays]


def cost(flops, moved, transcendentals=0):
    return pl.CostEstimate(flops=flops, bytes_accessed=moved, transcendentals=transcendentals)


def place():
    return lax.axis_index("tp"), lax.rem(lax.axis_index("queue"), 2)


def row_and_column():
    slot = lax.axis_index("queue")
    return lax.div(slot, 16), lax.rem(lax.div(slot, 2), 4)


def slice_kernel(w, out, sem):
    side, core = place()
    row, _ = row_and_column()
    depth, width = out.shape[1:]
    base = (1 - side) * (RING * width)
    source = pl.ds(pl.multiple_of(core * depth, depth), depth)
    copies = []
    for i in range(2):
        cols = pl.ds(pl.multiple_of(base + lax.rem(row + 2 * i, RING) * width, width), width)
        copies.append(pltpu.make_async_copy(w.at[source, cols], out.at[i], sem.at[i]))
        copies[-1].start()
    for copy in copies:
        copy.wait()


def local(kernel, outs, specs, flops, moved, *args, scratch=(), limit=1 << 20):
    placed = []
    for spec, arg in zip(specs, args):
        if spec is IN_VMEM:
            arg = near_core(arg)[0]
        elif spec is IN_HBM:
            arg = far_away(arg)[0]
        placed.append(arg)
    return pl.pallas_call(
        kernel,
        out_shape=outs,
        in_specs=list(specs),
        out_specs=jax.tree.map(lambda _: IN_VMEM, outs),
        scratch_shapes=list(scratch),
        cost_estimate=cost(flops, moved),
        compiler_params=pltpu.CompilerParams(vmem_limit_bytes=limit),
    )(*placed)


def prepare_kernel(
    step, keep, noise, level, text, mods, coefs, row, words, ints, reals, sem
):
    first = pltpu.make_async_copy(step, ints, sem.at[0])
    small = [pltpu.make_async_copy(source, reals.at[i], sem.at[1 + i]) for i, source in enumerate((keep, noise))]
    small.append(pltpu.make_async_copy(text, words, sem.at[3]))
    first.start()
    for copy in small:
        copy.start()
    first.wait()
    at = ints[0]
    level_copy = pltpu.make_async_copy(level.at[pl.ds(at, 1)], row, sem.at[4])
    level_copy.start()
    for copy in small:
        copy.wait()
    for i in range(2):
        coefs[i : i + 1, :] = jnp.full((1, coefs.shape[1]), reals[i, at], F32)
    level_copy.wait()
    for branch in range(2):
        mods[branch : branch + 1, :] = row[0, 0:1, :] + words[branch, 0:1, :]
        mods[2 + branch : 3 + branch, :] = 1.0 + (row[0, 1:2, :] + words[branch, 1:2, :])


def home_kernel(native, foreign, mods, coefs, w, out, normed, kept):
    half = foreign.shape[1]
    tokens = foreign.shape[0]
    side, _ = place()
    total = 2 * half
    parts = (native[0].astype(F32), foreign[...].astype(F32))
    mean = sum(jnp.sum(p, axis=-1, keepdims=True) for p in parts) / total
    parts = tuple(p - mean for p in parts)
    spread = sum(jnp.sum(p * p, axis=-1, keepdims=True) for p in parts) / total
    inverse = lax.rsqrt(spread + EPSILON)
    for part, where in zip(parts, (side, 1 - side)):
        unit = part * inverse
        cols = pl.ds(pl.multiple_of(where * half, half), half)
        for branch in range(2):
            shift = mods[branch : branch + 1, cols]
            gain = mods[2 + branch : 3 + branch, cols]
            normed[branch * tokens : (branch + 1) * tokens, cols] = (unit * gain + shift).astype(BF16)
    products(normed, w, 1, out, (1,))
    kept[...] = (coefs[0:1, 0:1] * native[0].astype(F32)).astype(BF16)


def products(normed, w, first, out, flip=()):
    width = out.shape[2] // GROUPS
    for i in range(out.shape[0]):
        for g in range(GROUPS):
            cols = slice(g * width, (g + 1) * width)
            value = jnp.dot(normed[...], w[first + i, :, cols], preferred_element_type=F32)
            out[i, :, cols] = (value.T if i in flip else value).astype(BF16)


def query_kernel(normed, w, w_out, back, ahead, out, columns, table, sem):
    side, _ = place()
    half = columns.shape[1]
    cols = pl.ds(pl.multiple_of(side * half, half), half)
    copy = pltpu.make_async_copy(w_out.at[:, cols], columns, sem)
    copy.start()
    count = lax.axis_size("queue")
    frame = lax.axis_index("queue")
    sense = 1 - 2 * lax.rem(frame, 2)
    for i, distance in enumerate((0, 1, -1, -2, 2)):
        offset = sense * distance
        target = frame + offset
        allowed = (offset >= -back[0]) & (offset <= ahead[0]) & (target >= 0) & (target < count)
        entry = jnp.where(allowed, 0.0, -1e30).astype(F32)
        table[i : i + 1, :] = jnp.full((1, table.shape[1]), entry, F32)
    products(normed, w, 0, out)
    copy.wait()


def scored(table, q, keys, which, branch, g):
    width = q.shape[2] // GROUPS
    cols = slice(g * width, (g + 1) * width)
    tokens = q.shape[1] // 2
    at = slice(branch * tokens, (branch + 1) * tokens)
    heads = width // HDIM
    lane_head = lax.broadcasted_iota(jnp.int32, (1, width), 1) // HDIM
    keys = jnp.concatenate([key[at, cols] for key in keys], axis=0)
    query = q[0, at, cols] * jnp.asarray(HDIM ** (-0.5), BF16)
    stacked = jnp.concatenate(
        [jnp.where(lane_head == h, query, jnp.zeros_like(query)) for h in range(heads)], axis=0
    )
    scores = lax.dot_general(keys, stacked, (((1,), (1,)), ((), ())), preferred_element_type=F32)
    return jnp.concatenate(
        [scores[i * tokens : (i + 1) * tokens] + table[w : w + 1, :] for i, w in enumerate(which)], axis=0
    )


def flipped(tokens, width, branch, g):
    return slice(g * width + branch * tokens, g * width + (branch + 1) * tokens)


def first_kernel(table, q, own, mate, close, passed, sums, tops, totals):
    tokens = q.shape[1] // 2
    width = q.shape[2] // GROUPS
    for g in range(GROUPS):
        for branch in range(2):
            scores = scored(table, q, [block.at[0] for block in (own, mate, close, passed)], (0, 1, 2, 4), branch, g)
            at = flipped(tokens, width, branch, g)
            values = jnp.concatenate([block[1, :, at] for block in (own, mate, close, passed)], axis=1)
            top = jnp.max(scores, axis=0, keepdims=True)
            expon = jnp.exp(scores - top)
            spot = 2 * g + branch
            sums[spot] = jnp.dot(values, expon.astype(BF16), preferred_element_type=F32)
            tops[spot : spot + 1, :] = top
            totals[spot : spot + 1, :] = jnp.sum(expon, axis=0, keepdims=True)


def second_kernel(table, q, far, tops, totals, weights, scales):
    for g in range(GROUPS):
        for branch in range(2):
            spot = 2 * g + branch
            scores = scored(table, q, [far.at[0]], (3,), branch, g)
            before = tops[spot : spot + 1, :]
            top = jnp.maximum(before, jnp.max(scores, axis=0, keepdims=True))
            expon = jnp.exp(scores - top)
            old = jnp.exp(before - top)
            scale = 1.0 / (old * totals[spot : spot + 1, :] + jnp.sum(expon, axis=0, keepdims=True))
            weights[spot] = expon.astype(BF16)
            scales[spot : spot + 1, :] = scale
            scales[8 + spot : 9 + spot, :] = old * scale


def third_kernel(coefs, far, weights, scales, sums, out):
    width = out.shape[1] // GROUPS
    tokens = out.shape[0]
    noise = coefs[1:2, 0:1]
    for g in range(GROUPS):
        results = []
        for branch in range(2):
            spot = 2 * g + branch
            values = far[1, :, flipped(tokens, width, branch, g)]
            fresh = jnp.dot(values, weights[spot], preferred_element_type=F32)
            picked = []
            for h in range(width // HDIM):
                dims, lanes = slice(h * HDIM, (h + 1) * HDIM), slice(h * tokens, (h + 1) * tokens)
                mixed = scales[8 + spot : 9 + spot, lanes] * sums[spot, dims, lanes]
                mixed = mixed + scales[spot : spot + 1, lanes] * fresh[dims, lanes]
                picked.append(mixed.astype(BF16).astype(F32))
            results.append(jnp.concatenate(picked, axis=0))
        cond, plain = results
        out[:, g * width : (g + 1) * width] = (-noise * (plain + GUIDANCE * (cond - plain))).T.astype(BF16)


def early_kernel(before, other, *refs):
    *pieces, out = refs
    _, core = place()
    row, column = row_and_column()
    block, part = pieces[0].shape[1:]
    low, high = other[:, :block], other[:, block:]
    halves = (jnp.where(core == 0, low, high), jnp.where(core == 0, high, low))
    beside = jnp.where(column >= 2, RING - 1, 1)
    for i, turn in enumerate((0, 2, beside, beside + 2)):
        cols = pl.ds(pl.multiple_of(lax.rem(row + turn, RING) * part, part), part)
        total = before[:, cols].astype(F32)
        for half, piece in zip(halves, pieces[2 * (i // 2) : 2 * (i // 2) + 2]):
            total = total + jnp.dot(half, piece[i % 2], preferred_element_type=F32)
        out[:, cols] = total


def final_kernel(early, mix, own, out, held, sem):
    step = held.shape[1] // GROUPS
    copies = []
    for i in range(GROUPS):
        cols = slice(i * step, (i + 1) * step)
        held[:, cols] = (early[:, cols] + jnp.dot(mix[...], own[:, cols], preferred_element_type=F32)).astype(BF16)
        copies.append(pltpu.make_async_copy(held.at[:, cols], out.at[0, :, cols], sem.at[i]))
        copies[-1].start()
    for copy in copies:
        copy.wait()


def body(
    latent,
    step_index,
    back_reach,
    ahead_reach,
    level_mod,
    text_mod,
    w_qkv,
    w_out,
    keep_coef,
    noise_coef,
):
    count = lax.axis_size("queue")
    every = range(count)
    onward = [(s, (s + 1) % count) for s in every]
    across = [(2 * s + t, 2 * ((s + 1) % count) + 1 - t) for s in every for t in range(2)]
    mates = [(s, s ^ 1) for s in every]
    near = [(s, s + 1 if s % 2 else s - 1) for s in every]
    far = [(s, s - 2 if s % 2 else s + 2) for s in every]
    near, far = ([(s, d) for s, d in pairs if 0 <= d < count] for pairs in (near, far))
    swap = [(0, 1), (1, 0)]
    tokens = latent.shape[1]
    half = latent.shape[2]

    def send(value, axis, pairs):
        return lax.ppermute(value, axis, pairs)

    width = w_qkv.shape[2]
    rows = 2 * tokens
    full = 2 * half
    heads = width // (GROUPS * HDIM)
    kv_shape = VMEM((2, rows, width), BF16)
    normed_shape = VMEM((rows, full), BF16)
    sems = lambda n: pltpu.SemaphoreType.DMA((n,))
    sem = pltpu.SemaphoreType.DMA
    work = 4 * rows * full * width

    ring = []
    for slot in every:
        step = 16 if (slot // 2) % 4 >= 2 else -16
        ring.append((slot, (slot + step) % count))
    mirror = [(2 * slot + t, 2 * (slot ^ 8) + 1 - t) for slot in every for t in range(2)]
    foreign = send(latent[0], "tp", swap)
    mods, coefs = local(
        prepare_kernel,
        (
            VMEM((4, full), F32), VMEM((8, 128), F32),
        ),
        (LOOSE,) + (IN_HBM,) * 4, BUSY, 4 * w_qkv.size,
        step_index, keep_coef, noise_coef, level_mod, text_mod,
        scratch=(
            VMEM((1, 2, full), F32), VMEM((2, 2, full), F32), pltpu.SMEM((1,), jnp.int32),
            pltpu.SMEM((2, keep_coef.shape[0]), F32), sems(5),
        ),
    )
    sliced = local(
        slice_kernel, VMEM((2, width // 2, half // RING), BF16), (IN_HBM,), BUSY, 2 * w_out.size, w_out,
        scratch=(sems(2),),
    )
    across_rows = send(sliced, ("queue", "tp"), mirror)
    beside_rows = send(across_rows, "queue", ring)
    remote = (across_rows, send(across_rows, "queue", mates), beside_rows, send(beside_rows, "queue", mates))
    kv, normed, scaled = local(
        home_kernel, (kv_shape, normed_shape, VMEM((tokens, half), BF16)), (IN_VMEM,) * 5, work, 4 * w_qkv.size,
        latent, foreign, mods, coefs, w_qkv, limit=12 << 20,
    )
    before = send(scaled, "queue", onward)
    near_kv = send(kv, "queue", near)
    mate_kv = send(kv, "queue", mates)
    far_kv = send(mate_kv, "queue", near)
    passed_kv = send(near_kv, "queue", mates)
    q, w_columns, table = local(
        query_kernel, (VMEM((1, rows, width), BF16), VMEM((width, half), BF16), VMEM((8, heads * tokens), F32)),
        (IN_VMEM, IN_VMEM, IN_HBM, IN_SMEM, IN_SMEM), work // 2, 2 * w_qkv.size, normed, w_qkv, w_out,
        back_reach, ahead_reach, scratch=(sem,), limit=12 << 20,
    )
    pairs = 2 * GROUPS
    sums, tops, totals = local(
        first_kernel,
        (
            VMEM((pairs, width // GROUPS, heads * tokens), F32), VMEM((8, heads * tokens), F32),
            VMEM((8, heads * tokens), F32),
        ),
        (IN_VMEM,) * 6, work, 32 * rows * width, table, q, kv, mate_kv, near_kv, passed_kv, limit=12 << 20,
    )
    chances, scales = local(
        second_kernel, (VMEM((pairs, tokens, heads * tokens), BF16), VMEM((16, heads * tokens), F32)),
        (IN_VMEM,) * 5, work // 8, 16 * rows * width, table, q, far_kv, tops, totals, limit=12 << 20,
    )
    mix = local(
        third_kernel, VMEM((tokens, width), BF16), (IN_VMEM,) * 5, work // 8, 16 * rows * width,
        coefs, far_kv, chances, scales, sums, limit=12 << 20,
    )
    mix_there = send(mix, ("queue", "tp"), across)
    mix_here = send(mix, "queue", onward)
    early = local(
        early_kernel, VMEM((tokens, half), F32), (IN_VMEM,) * 6, 2 * tokens * width * half, 4 * width * half,
        before, mix_there, *remote, limit=8 << 20,
    )
    return pl.pallas_call(
        final_kernel,
        out_shape=jax.ShapeDtypeStruct((1, tokens, half), BF16),
        in_specs=[IN_VMEM] * 3,
        out_specs=LOOSE,
        scratch_shapes=[VMEM((tokens, half), BF16), sems(GROUPS)],
        cost_estimate=cost(2 * tokens * width * half, 4 * width * half),
        compiler_params=pltpu.CompilerParams(vmem_limit_bytes=8 << 20),
        name="final",
    )(*near_core(early, mix_here, w_columns))


def solution(mesh):
    return jax.shard_map(
        body,
        mesh=mesh,
        in_specs=(
            P("queue", None, "tp"),
            P("queue"),
            P("queue"),
            P("queue"),
            P(),
            P(),
            P(None, None, "tp"),
            P("tp", None),
            P(),
            P(),
        ),
        out_specs=P("queue", None, "tp"),
        check_vma=False,
    )
```
